32 devices in a mesh: groups: 2 (over x), ctx: 16 (over z, y, core).
Axes of the slice: x: 2, y: 2, z: 4, core: 2. Of those that a mesh axis runs over, the one named last changes fastest.
Arguments:
- queries: bfloat16 [16384, 2048], P(('groups', 'ctx')), parts along dimension 0, may hold values from -6 to 6
- keys: bfloat16 [256, 2048], P(('groups', 'ctx')), parts along dimension 0, may hold values from -6 to 6
- values: bfloat16 [256, 2048], P(('groups', 'ctx')), parts along dimension 0, may hold values from -6 to 6
- lengths: int32 [32], P(('groups', 'ctx')), parts along dimension 0, may hold values from 1 to 8, as said below
- dout: bfloat16 [16384, 2048], P(('groups', 'ctx')), parts along dimension 0, may hold values from -6 to 6
Outputs:
- attended: bfloat16 [16384, 2048], P(('groups', 'ctx')), parts along dimension 0
- query_grad: bfloat16 [16384, 2048], P(('groups', 'ctx')), parts along dimension 0
- key_grad: bfloat16 [256, 2048], P(('groups', 'ctx')), parts along dimension 0
- value_grad: bfloat16 [256, 2048], P(('groups', 'ctx')), parts along dimension 0
The draws below stay inside these ranges and needn't reach their ends.
There are 2 independent parts, one for each index of `groups`. The reference program is written for one: setup_inputs(seed, part) draws one part's arguments, and reference() takes and returns one part's arrays. A program takes and returns all parts, laid end to end along the dimension named above; each array names one. Nothing has to cross between parts.
Inputs may be any that keep to these rules, and one draw needn't show every extreme that they name: `lengths`: every shard has at least one live position; shard 0 is full.
All inputs are finite; a program needn't handle non-finite values.
Results may differ from the reference program's by a relative error of at most 0.0014.
The reference program's roundings to bfloat16 on the way count: a program that leaves them out, or rounds other values in their place, can miss the bound.
Values may be sent and summed in bfloat16 or wider, within the bound.
No kernel may reach another device: no remote copies, remote signals or barrier semaphores. Data moves between devices by JAX's collectives and lax.ppermute only.
A program may use at most 128 MiB of HBM per device.

```python
import jax
import jax.numpy as jnp
from jax import lax

HEADS = 32
HEAD_DIM = 64
MEM_DEV = 8
TOKENS = 8192
MEMORY = 128
N_CTX = 16


def draw_queries(key, part):
    shape_all = (TOKENS, HEADS * HEAD_DIM)
    sample_base = jax.random.normal(jax.random.fold_in(key, 11), shape_all)
    return jnp.clip(sample_base, -6.0, 6.0).astype(jnp.bfloat16)


def draw_keys(key, part):
    shape_all = (MEMORY, HEADS * HEAD_DIM)
    sample_base = jax.random.normal(jax.random.fold_in(key, 21), shape_all)
    return jnp.clip(sample_base, -6.0, 6.0).astype(jnp.bfloat16)


def draw_lengths(key, part):
    drawn = jax.random.randint(jax.random.fold_in(key, 31), (N_CTX,), 1, MEM_DEV + 1)
    return drawn.at[0].set(MEM_DEV).astype(jnp.int32)


def steps_of(key, dims, split, least, largest):
    def one(position, blocks):
        heights = jax.random.uniform(jax.random.fold_in(jax.random.fold_in(key, 6), position), (blocks,), jnp.float32, least / len(split), largest / len(split))
        return jnp.repeat(jnp.exp(heights), dims[position] // blocks).reshape((-1,) + (1,) * (len(dims) - position - 1))

    level = one(*split[0])
    for cut in split[1:]:
        level = level * one(*cut)
    return level


def scatter_about(rng, dims, spread, bound, cuts=(), kind=jnp.bfloat16):
    level = steps_of(rng, dims, cuts, -0.22, 0.18) if cuts else 1.0
    values = jax.random.normal(rng, dims, jnp.float32) * spread * level
    return jnp.minimum(jnp.maximum(values, -bound), bound).astype(kind)


def setup_inputs(seed: int = 0, part: int = 0) -> dict:
    seeds = jax.random.split(jax.random.key(seed), 6)
    part_splits = jax.random.split(jax.random.fold_in(seeds[5], part), 6)
    queries = draw_queries(jax.random.fold_in(jax.random.fold_in(seeds[5], part), 71), part)
    keys = draw_keys(jax.random.fold_in(jax.random.fold_in(seeds[5], part), 71), part)
    values = scatter_about(part_splits[2], (MEMORY, HEADS * HEAD_DIM), 1.0, 6.0, ((0, 16),))
    lengths = draw_lengths(jax.random.fold_in(jax.random.fold_in(seeds[5], part), 71), part)
    dout = scatter_about(part_splits[4], (TOKENS, HEADS * HEAD_DIM), 1.0, 6.0, ((0, 16),))
    return dict(queries=queries, keys=keys, values=values, lengths=lengths, dout=dout)


neg_fill = -1.0e30


def reference(queries, keys, values, lengths, dout):
    width = HEADS * HEAD_DIM
    factor = HEAD_DIM ** -0.5
    positions = jnp.arange(MEMORY, dtype=jnp.int32)
    limits = jnp.repeat(lengths.astype(jnp.int32), MEM_DEV)
    usable = (positions % MEM_DEV) < limits

    def heads_first(block):
        return block.reshape(block.shape[0], HEADS, HEAD_DIM).transpose(1, 0, 2)

    def heads_back(block):
        return block.transpose(1, 0, 2).reshape(block.shape[1], width)

    def per_head(pieces):
        query_h, key_h, value_h, grad_h = pieces
        logits = jnp.dot(query_h, key_h.T, preferred_element_type=jnp.float32) * factor
        logits = jnp.where(usable[None, :], logits, neg_fill)
        row_max = jnp.max(logits, axis=1, keepdims=True)
        expo_w = jnp.exp(logits - row_max)
        softmax_w = expo_w / jnp.sum(expo_w, axis=1, keepdims=True)
        weights_low = softmax_w.astype(jnp.bfloat16)
        attended = jnp.dot(weights_low, value_h, preferred_element_type=jnp.float32).astype(jnp.bfloat16)
        delta = jnp.sum(grad_h.astype(jnp.float32) * attended.astype(jnp.float32), axis=1, keepdims=True)
        grad_p = jnp.dot(grad_h, value_h.T, preferred_element_type=jnp.float32)
        grad_s = (softmax_w * (grad_p - delta)).astype(jnp.bfloat16)
        query_grad = (jnp.dot(grad_s, key_h, preferred_element_type=jnp.float32) * factor).astype(jnp.bfloat16)
        key_grad = (jnp.dot(grad_s.T, query_h, preferred_element_type=jnp.float32) * factor).astype(jnp.bfloat16)
        value_grad = jnp.dot(weights_low.T, grad_h, preferred_element_type=jnp.float32).astype(jnp.bfloat16)
        return attended, query_grad, key_grad, value_grad

    results = lax.map(per_head, (heads_first(queries), heads_first(keys), heads_first(values), heads_first(dout)))
    return (heads_back(results[0]), heads_back(results[1]), heads_back(results[2]), heads_back(results[3]))
```

```python
import jax
import jax.numpy as jnp
from jax import lax
from jax.experimental import pallas as pl
from jax.experimental.pallas import tpu as pltpu
from jax.sharding import PartitionSpec as P

HEAD_DIM = 64
LANES = 128
SCALE = HEAD_DIM ** -0.5
NEG = -1e30
F32 = jnp.float32
BF16 = jnp.bfloat16

CHUNKS = (1.0,)
PAIRS_PER_STEP = 4


def dot(a, b, ca, cb):
    return lax.dot_general(a, b, (((ca,), (cb,)), ((), ())), preferred_element_type=F32)


def pair_pass(q, do, k2, v2, bias, tokens, memory):
    s = dot(k2, q, 1, 1).reshape(2, memory, tokens) + bias
    e = jnp.exp(s - jnp.max(s, axis=1, keepdims=True))
    p = e * (1.0 / jnp.sum(e, axis=1, keepdims=True))
    p_low = p.astype(BF16).reshape(2 * memory, tokens)
    att = dot(v2, p_low, 0, 0).astype(BF16)
    grad_p = dot(v2, do, 1, 1).reshape(2, memory, tokens)
    delta = (do.T.astype(F32) * att.astype(F32)).reshape(2, HEAD_DIM, tokens)
    delta = jnp.sum(delta, axis=1, keepdims=True)
    grad_s = (p * (grad_p - delta)).astype(BF16).reshape(2 * memory, tokens)
    dq = dot(k2, grad_s, 0, 0).astype(BF16)
    return att.T, dq.T, dot(grad_s, q, 1, 0), dot(p_low, do, 1, 0)


def attention(queries, dout, first, second, carried, offset, pairs):
    tokens, width = queries.shape
    half = first.shape[0]
    memory = 2 * half
    step = max(d for d in range(1, PAIRS_PER_STEP + 1) if pairs % d == 0 and offset % d == 0)
    grid = pairs // step
    block = step * LANES

    def body(*refs):
        q_ref, do_ref, ka_ref, kb_ref, va_ref, vb_ref, fa_ref, fb_ref = refs[:8]
        att_ref, dq_ref, lo_ref, hi_ref = refs[-4:]
        live = jnp.concatenate([fa_ref[...], fb_ref[...]], axis=0).astype(F32)
        bias = jnp.where(live[:, :1] > 0, 0.0, NEG)
        left = lax.broadcasted_iota(jnp.int32, (memory, LANES), 1) < HEAD_DIM
        zero = jnp.zeros((memory, LANES), BF16)

        def both(x):
            return jnp.concatenate([jnp.where(left, x, zero), jnp.where(left, zero, x)], axis=0)

        for i in range(step):
            c = pl.ds(i * LANES, LANES)
            k = jnp.concatenate([ka_ref[:, c], kb_ref[:, c]], axis=0) * jnp.asarray(SCALE, BF16)
            v = jnp.concatenate([va_ref[:, c], vb_ref[:, c]], axis=0)
            att, dq, dk, dv = pair_pass(q_ref[:, c], do_ref[:, c], both(k), both(v), bias, tokens, memory)
            att_ref[:, c] = att
            dq_ref[:, c] = dq
            dk = jnp.where(left, dk[:memory], dk[memory:]) * SCALE
            dv = jnp.where(left, dv[:memory], dv[memory:])
            for j, x in enumerate((dk, dv)):
                c2 = pl.ds((2 * i + j) * LANES, LANES)
                lo_ref[:, c2] = x[:half]
                hi_ref[:, c2] = x[half:]

    base = offset // step
    token_spec = pl.BlockSpec((tokens, block), lambda g: (0, g + base))
    k_spec = pl.BlockSpec((half, block), lambda g: (0, g))
    v_spec = pl.BlockSpec((half, block), lambda g: (0, g + grid))
    flag_spec = pl.BlockSpec((half, LANES), lambda g: (0, 2 * pairs))
    term_spec = pl.BlockSpec((half, 2 * block), lambda g: (0, g))
    extra = () if carried is None else tuple(carried)
    return pl.pallas_call(
        body,
        grid=(grid,),
        in_specs=[token_spec, token_spec, k_spec, k_spec, v_spec, v_spec, flag_spec, flag_spec]
        + [pl.BlockSpec(memory_space=pl.ANY)] * len(extra),
        out_specs=[token_spec, token_spec, term_spec, term_spec],
        out_shape=[jax.ShapeDtypeStruct((tokens, width), BF16)] * 2
        + [jax.ShapeDtypeStruct((half, 2 * pairs * LANES), F32)] * 2,
        input_output_aliases={8 + i: i for i in range(len(extra))},
        compiler_params=pltpu.CompilerParams(
            dimension_semantics=("arbitrary",), vmem_limit_bytes=48 * 2**20
        ),
    )(queries, dout, first, second, first, second, first, second, *extra)


def split_pairs(total):
    ends, done = [0], 0.0
    for share in CHUNKS:
        done += share
        ends.append(min(total, round(done * total)))
    ends[-1] = total
    return [(a, b - a) for a, b in zip(ends, ends[1:]) if b > a]


def solution(mesh):
    n = mesh.shape["ctx"]
    bits = [1 << b for b in range(n.bit_length() - 1)]
    assert n == 1 << len(bits)

    def swap(x, bit):
        return lax.ppermute(x, "ctx", [(i, i ^ bit) for i in range(n)])

    def gather(x):
        for bit in bits[:0:-1]:
            x = jnp.concatenate([x, swap(x, bit)], axis=0)
        return x, swap(x, bits[0])

    def scatter(lo, hi):
        x = lo + swap(hi, bits[0])
        for bit in bits[1:]:
            half = x.shape[0] // 2
            x = x[:half] + swap(x[half:], bit)
        return x

    def per_device(queries, keys, values, lengths, dout):
        rows, width = keys.shape
        live = lax.broadcasted_iota(jnp.int32, (rows, LANES), 0) < lengths[0]
        chunks = split_pairs(width // LANES)
        gathered = []
        for start, pairs in chunks:
            cols = slice(start * LANES, (start + pairs) * LANES)
            packed = jnp.concatenate([keys[:, cols], values[:, cols], live.astype(BF16)], axis=1)
            gathered.append(gather(packed))
        carried, sums = None, []
        for (start, pairs), (first, second) in zip(chunks, gathered):
            *carried, lo, hi = attention(queries, dout, first, second, carried, start, pairs)
            sums.append(scatter(lo, hi))
        total = jnp.concatenate(sums, axis=1).reshape(rows, width // LANES, 2, LANES)
        key_grad = total[:, :, 0].reshape(rows, width).astype(BF16)
        value_grad = total[:, :, 1].reshape(rows, width).astype(BF16)
        return (*carried, key_grad, value_grad)

    spec = P(("groups", "ctx"), None)
    return jax.shard_map(
        per_device,
        mesh=mesh,
        in_specs=(spec, spec, spec, P(("groups", "ctx")), spec),
        out_specs=(spec,) * 4,
        check_vma=False,
    )
```

```python
import jax
import jax.numpy as jnp
from jax import lax
from jax.experimental import pallas as pl
from jax.experimental.pallas import tpu as pltpu
from jax.sharding import PartitionSpec as P

HEAD_DIM = 64
LANES = 128
SCALE = HEAD_DIM ** -0.5
NEG = -1e30
F32 = jnp.float32
BF16 = jnp.bfloat16

CHUNKS = (((8 / 16,), 0), ((8 / 16,), 1))
PAIRS_PER_STEP = 4
COST = 1
TIE = False


def dot(a, b, ca, cb):
    return lax.dot_general(a, b, (((ca,), (cb,)), ((), ())), preferred_element_type=F32)


def pair_pass(q, do, k2, v2, bias, tokens, memory):
    s = dot(k2, q, 1, 1).reshape(2, memory, tokens) + bias
    e = jnp.exp(s - jnp.max(s, axis=1, keepdims=True))
    p = e * (1.0 / jnp.sum(e, axis=1, keepdims=True))
    p_low = p.astype(BF16).reshape(2 * memory, tokens)
    att = dot(v2, p_low, 0, 0).astype(BF16)
    grad_p = dot(v2, do, 1, 1).reshape(2, memory, tokens)
    delta = (do.T.astype(F32) * att.astype(F32)).reshape(2, HEAD_DIM, tokens)
    delta = jnp.sum(delta, axis=1, keepdims=True)
    grad_s = (p * (grad_p - delta)).astype(BF16).reshape(2 * memory, tokens)
    dq = dot(k2, grad_s, 0, 0).astype(BF16)
    return att.T, dq.T, dot(grad_s, q, 1, 0), dot(p_low, do, 1, 0)


def attention(queries, dout, first, second, results, terms, offset, place, pairs, total):
    tokens, width = queries.shape
    half = first.shape[0]
    memory = 2 * half
    most = max(1, PAIRS_PER_STEP * 128 // memory)
    step = max(d for d in range(1, most + 1) if all(x % d == 0 for x in (pairs, offset, place, total)))
    block = step * LANES

    def body(*refs):
        q_ref, do_ref, ka_ref, kb_ref, va_ref, vb_ref, fa_ref, fb_ref = refs[:8]
        att_ref, dq_ref, lo_ref, hi_ref = refs[-4:]
        live = jnp.concatenate([fa_ref[...], fb_ref[...]], axis=0).astype(F32)
        bias = jnp.where(live[:, :1] > 0, 0.0, NEG)
        left = lax.broadcasted_iota(jnp.int32, (memory, LANES), 1) < HEAD_DIM
        zero = jnp.zeros((memory, LANES), BF16)

        def both(x):
            return jnp.concatenate([jnp.where(left, x, zero), jnp.where(left, zero, x)], axis=0)

        for i in range(step):
            c = pl.ds(i * LANES, LANES)
            k = jnp.concatenate([ka_ref[:, c], kb_ref[:, c]], axis=0) * jnp.asarray(SCALE, BF16)
            v = jnp.concatenate([va_ref[:, c], vb_ref[:, c]], axis=0)
            att, dq, dk, dv = pair_pass(q_ref[:, c], do_ref[:, c], both(k), both(v), bias, tokens, memory)
            att_ref[:, c] = att
            dq_ref[:, c] = dq
            dk = jnp.where(left, dk[:memory], dk[memory:]) * SCALE
            dv = jnp.where(left, dv[:memory], dv[memory:])
            tc = pl.ds(2 * i * LANES, 2 * LANES)
            lo_ref[:, tc] = jnp.concatenate([dk[:half], dv[:half]], axis=1)
            hi_ref[:, tc] = jnp.concatenate([dk[half:], dv[half:]], axis=1)

    def cols(rows, width, start):
        return pl.BlockSpec((rows, width), lambda g: (0, g + start))

    token_spec = cols(tokens, block, offset // step)
    k_spec = cols(half, block, place // step)
    v_spec = cols(half, block, (total + place) // step)
    flag_spec = pl.BlockSpec((half, LANES), lambda g: (0, 2 * total))
    term_spec = cols(half, 2 * block, place // step)
    extra = {}
    if results is not None:
        extra.update(enumerate(results))
    if terms is not None:
        extra.update(enumerate(terms, 2))
    scratch = min(52, 12 + step * memory * tokens * 2 * 4 * 4 // 2**20)
    return pl.pallas_call(
        body,
        grid=(pairs // step,),
        in_specs=[token_spec, token_spec, k_spec, k_spec, v_spec, v_spec, flag_spec, flag_spec]
        + [pl.BlockSpec(memory_space=pl.ANY)] * len(extra),
        out_specs=[token_spec, token_spec, term_spec, term_spec],
        out_shape=[jax.ShapeDtypeStruct((tokens, width), BF16)] * 2
        + [jax.ShapeDtypeStruct((half, 2 * total * LANES), F32)] * 2,
        input_output_aliases={8 + i: out for i, out in enumerate(extra)},
        compiler_params=pltpu.CompilerParams(
            dimension_semantics=("arbitrary",), vmem_limit_bytes=scratch * 2**20
        ),
        cost_estimate=pl.CostEstimate(
            flops=COST * pairs * 12 * tokens * 2 * memory * LANES,
            transcendentals=pairs * tokens * 2 * memory,
            bytes_accessed=pairs * LANES * 8 * (tokens + 2 * memory),
        ),
    )(queries, dout, first, second, first, second, first, second, *extra.values())


def split_pairs(total):
    chunks, done, share = [], 0, 0.0
    for shares, turn in CHUNKS:
        start, sizes = done, []
        for s in shares:
            share += s
            end = min(total, round(share * total))
            if end > done:
                sizes.append(end - done)
            done = end
        if sizes:
            chunks.append((start, sizes, turn))
    assert done == total
    return chunks


def solution(mesh):
    n = mesh.shape["ctx"]
    bits = [1 << b for b in range(n.bit_length() - 1)]
    assert n == 1 << len(bits)

    def reduce_order(turn):
        order = list(bits)
        if turn and len(order) > 2:
            order[1], order[2] = order[2], order[1]
        return order

    def swap(x, bit):
        return lax.ppermute(x, "ctx", [(i, i ^ bit) for i in range(n)])

    def gather(x, order):
        for bit in order[:-1]:
            x = jnp.concatenate([x, swap(x, bit)], axis=0)
        return x, swap(x, order[-1])

    def halve(x):
        half = x.shape[0] // 2
        return x[:half], x[half:]

    def per_device(queries, keys, values, lengths, dout):
        rows, width = keys.shape
        live = lax.broadcasted_iota(jnp.int32, (rows, LANES), 0) < lengths[0]
        chunks = split_pairs(width // LANES)
        gathered = []
        for start, sizes, turn in chunks:
            cols = slice(start * LANES, (start + sum(sizes)) * LANES)
            packed = jnp.concatenate([keys[:, cols], values[:, cols], live.astype(BF16)], axis=1)
            gathered.append(gather(packed, reduce_order(turn)[::-1]))
        results, sums, orders = None, [], []
        for (start, sizes, turn), (first, second) in zip(chunks, gathered):
            terms, place, total = None, 0, sum(sizes)
            for size in sizes:
                sent = []
                for j, order in enumerate(orders):
                    if order:
                        if TIE:
                            sums[j], results = lax.optimization_barrier((sums[j], results))
                        keep, send = sums[j] if isinstance(sums[j], (list, tuple)) else halve(sums[j])
                        sent.append((j, keep, swap(send, order.pop(0))))
                out = attention(queries, dout, first, second, results, terms, start + place, place, size, total)
                results, terms = out[:2], out[2:]
                place += size
                for j, keep, received in sent:
                    if TIE:
                        received, results = lax.optimization_barrier((received, results))
                    sums[j] = keep + received
            sums.append(terms)
            orders.append(reduce_order(turn))
        while any(orders):
            for j, order in enumerate(orders):
                if order:
                    keep, send = sums[j] if isinstance(sums[j], (list, tuple)) else halve(sums[j])
                    sums[j] = keep + swap(send, order.pop(0))
        total = jnp.concatenate(sums, axis=1).reshape(rows, width // LANES, 2, LANES)
        key_grad = total[:, :, 0].reshape(rows, width).astype(BF16)
        value_grad = total[:, :, 1].reshape(rows, width).astype(BF16)
        return (*results, key_grad, value_grad)

    spec = P(("groups", "ctx"), None)
    return jax.shard_map(
        per_device,
        mesh=mesh,
        in_specs=(spec, spec, spec, P(("groups", "ctx")), spec),
        out_specs=(spec,) * 4,
        check_vma=False,
    )
```

```python
import jax
import jax.numpy as jnp
from jax import lax
from jax.experimental import pallas as pl
from jax.experimental.pallas import tpu as pltpu
from jax.sharding import PartitionSpec as P

HEAD_DIM = 64
LANES = 128
SCALE = HEAD_DIM ** -0.5
NEG = -1e30
F32 = jnp.float32
BF16 = jnp.bfloat16

CHUNKS = (((8 / 16,), 0), ((8 / 16,), 1))
PAIRS_PER_STEP = 4
COST = 1
TIE = False


def dot(a, b, ca, cb):
    return lax.dot_general(a, b, (((ca,), (cb,)), ((), ())), preferred_element_type=F32)


def pair_pass(q, do, k2, v2, bias, tokens, memory):
    s = dot(k2, q, 1, 1).reshape(2, memory, tokens) + bias
    e = jnp.exp(s - jnp.max(s, axis=1, keepdims=True))
    p = e * (1.0 / jnp.sum(e, axis=1, keepdims=True))
    p_low = p.astype(BF16).reshape(2 * memory, tokens)
    att = dot(v2, p_low, 0, 0).astype(BF16)
    grad_p = dot(v2, do, 1, 1).reshape(2, memory, tokens)
    delta = (do.T.astype(F32) * att.astype(F32)).reshape(2, HEAD_DIM, tokens)
    delta = jnp.sum(delta, axis=1, keepdims=True)
    grad_s = (p * (grad_p - delta)).astype(BF16).reshape(2 * memory, tokens)
    dq = dot(k2, grad_s, 0, 0).astype(BF16)
    return att.T, dq.T, dot(grad_s, q, 1, 0), dot(p_low, do, 1, 0)


def attention(queries, dout, first, second, live, order, results, terms, offset, place, pairs, total):
    tokens, width = queries.shape
    half = first.shape[0]
    memory = 2 * half
    rows = memory // len(order)
    most = max(1, PAIRS_PER_STEP * 128 // memory)
    step = max(d for d in range(1, most + 1) if all(x % d == 0 for x in (pairs, offset, place, total)))
    block = step * LANES

    def body(*refs):
        q_ref, do_ref, ka_ref, kb_ref, va_ref, vb_ref, fa_ref, fb_ref = refs[:8]
        att_ref, dq_ref, lo_ref, hi_ref = refs[-4:]
        flags = jnp.concatenate([fa_ref[...], fb_ref[...]], axis=0).astype(F32)
        flags = jnp.concatenate([flags[at * rows : (at + 1) * rows, :1] for at in order], axis=0)
        bias = jnp.where(flags > 0, 0.0, NEG)
        left = lax.broadcasted_iota(jnp.int32, (memory, LANES), 1) < HEAD_DIM
        zero = jnp.zeros((memory, LANES), BF16)

        def both(x):
            return jnp.concatenate([jnp.where(left, x, zero), jnp.where(left, zero, x)], axis=0)

        for i in range(step):
            c = pl.ds(i * LANES, LANES)
            k = jnp.concatenate([ka_ref[:, c], kb_ref[:, c]], axis=0) * jnp.asarray(SCALE, BF16)
            v = jnp.concatenate([va_ref[:, c], vb_ref[:, c]], axis=0)
            att, dq, dk, dv = pair_pass(q_ref[:, c], do_ref[:, c], both(k), both(v), bias, tokens, memory)
            att_ref[:, c] = att
            dq_ref[:, c] = dq
            dk = jnp.where(left, dk[:memory], dk[memory:]) * SCALE
            dv = jnp.where(left, dv[:memory], dv[memory:])
            tc = pl.ds(2 * i * LANES, 2 * LANES)
            lo_ref[:, tc] = jnp.concatenate([dk[:half], dv[:half]], axis=1)
            hi_ref[:, tc] = jnp.concatenate([dk[half:], dv[half:]], axis=1)

    def cols(rows, width, start):
        return pl.BlockSpec((rows, width), lambda g: (0, g + start))

    token_spec = cols(tokens, block, offset // step)
    k_spec = cols(half, block, place // step)
    v_spec = cols(half, block, (total + place) // step)
    flag_spec = pl.BlockSpec((half, LANES), lambda g: (0, live[0].shape[1] // LANES - 1))
    term_spec = cols(half, 2 * block, place // step)
    extra = {}
    if results is not None:
        extra.update(enumerate(results))
    if terms is not None:
        extra.update(enumerate(terms, 2))
    scratch = min(52, 12 + step * memory * tokens * 2 * 4 * 4 // 2**20)
    return pl.pallas_call(
        body,
        grid=(pairs // step,),
        in_specs=[token_spec, token_spec, k_spec, k_spec, v_spec, v_spec, flag_spec, flag_spec]
        + [pl.BlockSpec(memory_space=pl.ANY)] * len(extra),
        out_specs=[token_spec, token_spec, term_spec, term_spec],
        out_shape=[jax.ShapeDtypeStruct((tokens, width), BF16)] * 2
        + [jax.ShapeDtypeStruct((half, 2 * total * LANES), F32)] * 2,
        input_output_aliases={8 + i: out for i, out in enumerate(extra)},
        compiler_params=pltpu.CompilerParams(
            dimension_semantics=("arbitrary",), vmem_limit_bytes=scratch * 2**20
        ),
        cost_estimate=pl.CostEstimate(
            flops=COST * pairs * 12 * tokens * 2 * memory * LANES,
            transcendentals=pairs * tokens * 2 * memory,
            bytes_accessed=pairs * LANES * 8 * (tokens + 2 * memory),
        ),
    )(queries, dout, first, second, first, second, *live, *extra.values())


def split_pairs(total):
    chunks, done, share = [], 0, 0.0
    for shares, turn in CHUNKS:
        start, sizes = done, []
        for s in shares:
            share += s
            end = min(total, round(share * total))
            if end > done:
                sizes.append(end - done)
            done = end
        if sizes:
            chunks.append((start, sizes, turn))
    assert done == total
    return chunks


def solution(mesh):
    n = mesh.shape["ctx"]
    bits = [1 << b for b in range(n.bit_length() - 1)]
    assert n == 1 << len(bits)

    def reduce_order(turn):
        order = list(bits)
        if turn and len(order) > 2:
            order[1], order[2] = order[2], order[1]
        return order

    def swap(x, bit):
        return lax.ppermute(x, "ctx", [(i, i ^ bit) for i in range(n)])

    def gather(x, order):
        for bit in order[:-1]:
            x = jnp.concatenate([x, swap(x, bit)], axis=0)
        return x, swap(x, order[-1])

    def places(order):
        return [sum(b for i, b in enumerate(order) if j >> i & 1) for j in range(n)]

    def halve(x):
        half = x.shape[0] // 2
        return x[:half], x[half:]

    def per_device(queries, keys, values, lengths, dout):
        rows, width = keys.shape
        live = lax.broadcasted_iota(jnp.int32, (rows, LANES), 0) < lengths[0]
        chunks = split_pairs(width // LANES)
        gathered = []
        for start, sizes, turn in chunks:
            cols = slice(start * LANES, (start + sum(sizes)) * LANES)
            packed = [keys[:, cols], values[:, cols]] + ([] if gathered else [live.astype(BF16)])
            gathered.append(gather(jnp.concatenate(packed, axis=1), reduce_order(turn)[::-1]))
        flag_places = places(reduce_order(chunks[0][2])[::-1])
        results, sums, orders = None, [], []
        for (start, sizes, turn), (first, second) in zip(chunks, gathered):
            terms, place, total = None, 0, sum(sizes)
            at = [flag_places.index(p) for p in places(reduce_order(turn)[::-1])]
            for size in sizes:
                sent = []
                for j, order in enumerate(orders):
                    if order:
                        if TIE:
                            sums[j], results = lax.optimization_barrier((sums[j], results))
                        keep, send = sums[j] if isinstance(sums[j], (list, tuple)) else halve(sums[j])
                        sent.append((j, keep, swap(send, order.pop(0))))
                out = attention(
                    queries, dout, first, second, gathered[0], at, results, terms, start + place, place, size, total
                )
                results, terms = out[:2], out[2:]
                place += size
                for j, keep, received in sent:
                    if TIE:
                        received, results = lax.optimization_barrier((received, results))
                    sums[j] = keep + received
            sums.append(terms)
            orders.append(reduce_order(turn))
        while any(orders):
            for j, order in enumerate(orders):
                if order:
                    keep, send = sums[j] if isinstance(sums[j], (list, tuple)) else halve(sums[j])
                    sums[j] = keep + swap(send, order.pop(0))
        total = jnp.concatenate(sums, axis=1).reshape(rows, width // LANES, 2, LANES)
        key_grad = total[:, :, 0].reshape(rows, width).astype(BF16)
        value_grad = total[:, :, 1].reshape(rows, width).astype(BF16)
        return (*results, key_grad, value_grad)

    spec = P(("groups", "ctx"), None)
    return jax.shard_map(
        per_device,
        mesh=mesh,
        in_specs=(spec, spec, spec, P(("groups", "ctx")), spec),
        out_specs=(spec,) * 4,
        check_vma=False,
    )
```

```python
import jax
import jax.numpy as jnp
from jax import lax
from jax.experimental import pallas as pl
from jax.experimental.pallas import tpu as pltpu
from jax.sharding import PartitionSpec as P

HEAD_DIM = 64
LANES = 128
SCALE = HEAD_DIM ** -0.5
NEG = -1e30
F32 = jnp.float32
BF16 = jnp.bfloat16

CHUNKS = ((0.5, 0), (0.5, 1))
PAIRS_PER_STEP = 4


def dot(a, b, ca, cb):
    return lax.dot_general(a, b, (((ca,), (cb,)), ((), ())), preferred_element_type=F32)


def pair_pass(q, do, k2, v2, bias, tokens, memory):
    s = dot(k2, q, 1, 1).reshape(2, memory, tokens) + bias
    e = jnp.exp(s - jnp.max(s, axis=1, keepdims=True))
    p = e * (1.0 / jnp.sum(e, axis=1, keepdims=True))
    p_low = p.astype(BF16).reshape(2 * memory, tokens)
    att = dot(v2, p_low, 0, 0).astype(BF16)
    grad_p = dot(v2, do, 1, 1).reshape(2, memory, tokens)
    delta = (do.T.astype(F32) * att.astype(F32)).reshape(2, HEAD_DIM, tokens)
    delta = jnp.sum(delta, axis=1, keepdims=True)
    grad_s = (p * (grad_p - delta)).astype(BF16).reshape(2 * memory, tokens)
    dq = dot(k2, grad_s, 0, 0).astype(BF16)
    return att.T, dq.T, dot(grad_s, q, 1, 0), dot(p_low, do, 1, 0)


def attention(queries, dout, first, second, live, order, results, offset, pairs):
    tokens, width = queries.shape
    half = first.shape[0]
    memory = 2 * half
    rows = memory // len(order)
    most = max(1, PAIRS_PER_STEP * 128 // memory)
    step = max(d for d in range(1, most + 1) if all(x % d == 0 for x in (pairs, offset)))
    block = step * LANES

    def body(*refs):
        q_ref, do_ref, ka_ref, kb_ref, va_ref, vb_ref, fa_ref, fb_ref = refs[:8]
        att_ref, dq_ref, lo_ref, hi_ref = refs[-4:]
        flags = jnp.concatenate([fa_ref[...], fb_ref[...]], axis=0).astype(F32)
        flags = jnp.concatenate([flags[at * rows : (at + 1) * rows, :1] for at in order], axis=0)
        bias = jnp.where(flags > 0, 0.0, NEG)
        left = lax.broadcasted_iota(jnp.int32, (memory, LANES), 1) < HEAD_DIM
        zero = jnp.zeros((memory, LANES), BF16)

        def both(x):
            return jnp.concatenate([jnp.where(left, x, zero), jnp.where(left, zero, x)], axis=0)

        for i in range(step):
            c = pl.ds(i * LANES, LANES)
            k = jnp.concatenate([ka_ref[:, c], kb_ref[:, c]], axis=0) * jnp.asarray(SCALE, BF16)
            v = jnp.concatenate([va_ref[:, c], vb_ref[:, c]], axis=0)
            att, dq, dk, dv = pair_pass(q_ref[:, c], do_ref[:, c], both(k), both(v), bias, tokens, memory)
            att_ref[:, c] = att
            dq_ref[:, c] = dq
            dk = jnp.where(left, dk[:memory], dk[memory:]) * SCALE
            dv = jnp.where(left, dv[:memory], dv[memory:])
            tc = pl.ds(2 * i * LANES, 2 * LANES)
            lo_ref[:, tc] = jnp.concatenate([dk[:half], dv[:half]], axis=1)
            hi_ref[:, tc] = jnp.concatenate([dk[half:], dv[half:]], axis=1)

    def cols(rows, width, start):
        return pl.BlockSpec((rows, width), lambda g: (0, g + start))

    token_spec = cols(tokens, block, offset // step)
    k_spec = cols(half, block, 0)
    v_spec = cols(half, block, pairs // step)
    flag_spec = pl.BlockSpec((half, LANES), lambda g: (0, live[0].shape[1] // LANES - 1))
    term_spec = cols(half, 2 * block, 0)
    extra = results or ()
    scratch = min(52, 12 + step * memory * tokens * 2 * 4 * 4 // 2**20)
    return pl.pallas_call(
        body,
        grid=(pairs // step,),
        in_specs=[token_spec, token_spec, k_spec, k_spec, v_spec, v_spec, flag_spec, flag_spec]
        + [pl.BlockSpec(memory_space=pl.ANY)] * len(extra),
        out_specs=[token_spec, token_spec, term_spec, term_spec],
        out_shape=[jax.ShapeDtypeStruct((tokens, width), BF16)] * 2
        + [jax.ShapeDtypeStruct((half, 2 * pairs * LANES), F32)] * 2,
        input_output_aliases={8 + i: i for i in range(len(extra))},
        compiler_params=pltpu.CompilerParams(
            dimension_semantics=("arbitrary",), vmem_limit_bytes=scratch * 2**20
        ),
        cost_estimate=pl.CostEstimate(
            flops=pairs * 12 * tokens * 2 * memory * LANES,
            transcendentals=pairs * tokens * 2 * memory,
            bytes_accessed=pairs * LANES * 8 * (tokens + 2 * memory),
        ),
    )(queries, dout, first, second, first, second, *live, *extra)


def split_pairs(total):
    chunks, done, share = [], 0, 0.0
    for part, turn in CHUNKS:
        share += part
        end = min(total, round(share * total))
        if end > done:
            chunks.append((done, end - done, turn))
        done = end
    assert done == total
    return chunks


def solution(mesh):
    n = mesh.shape["ctx"]
    bits = [1 << b for b in range(n.bit_length() - 1)]
    assert n == 1 << len(bits)

    def reduce_order(turn):
        order = list(bits)
        if turn and len(order) > 2:
            order[1], order[2] = order[2], order[1]
        return order

    def swap(x, bit):
        return lax.ppermute(x, "ctx", [(i, i ^ bit) for i in range(n)])

    def gather(chunks, orders):
        chunks = list(chunks)
        for step in range(len(bits) - 1):
            before = None
            for k, order in enumerate(orders):
                received = swap(chunks[k], order[step])
                if before is not None:
                    received, _ = lax.optimization_barrier((received, before))
                chunks[k] = before = jnp.concatenate([chunks[k], received], axis=0)
        return [(x, swap(x, order[-1])) for x, order in zip(chunks, orders)]

    def places(order):
        return [sum(b for i, b in enumerate(order) if j >> i & 1) for j in range(n)]

    def scatter(keep, send, order):
        x = keep + swap(send, order[0])
        for bit in order[1:]:
            half = x.shape[0] // 2
            x = x[:half] + swap(x[half:], bit)
        return x

    def per_device(queries, keys, values, lengths, dout):
        rows, width = keys.shape
        chunks = split_pairs(width // LANES)
        orders = [reduce_order(turn) for _, _, turn in chunks]
        live = lax.broadcasted_iota(jnp.int32, (rows, LANES), 0) < lengths[0]
        packed = []
        for start, pairs, _ in chunks:
            cols = slice(start * LANES, (start + pairs) * LANES)
            parts = [keys[:, cols], values[:, cols]] + ([] if packed else [live.astype(BF16)])
            packed.append(jnp.concatenate(parts, axis=1))
        gathered = gather(packed, [order[::-1] for order in orders])
        flag_places = places(orders[0][::-1])
        results, sums = None, []
        for (start, pairs, _), order, (first, second) in zip(chunks, orders, gathered):
            tokens = (queries, dout)
            if not start:
                tokens = [pltpu.with_memory_space_constraint(x, pltpu.MemorySpace.HBM) for x in tokens]
            at = [flag_places.index(p) for p in places(order[::-1])]
            out = attention(*tokens,  first, second, gathered[0], at, results, start, pairs)
            results = out[:2]
            sums.append(scatter(*out[2:], order))
        total = jnp.concatenate(sums, axis=1).reshape(rows, width // LANES, 2, LANES)
        key_grad = total[:, :, 0].reshape(rows, width).astype(BF16)
        value_grad = total[:, :, 1].reshape(rows, width).astype(BF16)
        return (*results, key_grad, value_grad)

    spec = P(("groups", "ctx"), None)
    return jax.shard_map(
        per_device,
        mesh=mesh,
        in_specs=(spec, spec, spec, P(("groups", "ctx")), spec),
        out_specs=(spec,) * 4,
        check_vma=False,
    )
```

```python
import jax
import jax.numpy as jnp
from jax import lax
from jax.experimental import pallas as pl
from jax.experimental.pallas import tpu as pltpu
from jax.sharding import PartitionSpec as P

HEAD_DIM = 64
LANES = 128
SCALE = HEAD_DIM ** -0.5
NEG = -1e30
F32 = jnp.float32
BF16 = jnp.bfloat16

CHUNKS = ((0.5, 0), (0.5, 1))
PAIRS_PER_STEP = 4


def dot(a, b, ca, cb):
    return lax.dot_general(a, b, (((ca,), (cb,)), ((), ())), preferred_element_type=F32)


def attention(queries, dout, first, second, live, order, results, offset, pairs):
    tokens, width = queries.shape
    half = first.shape[0]
    memory = 2 * half
    rows = memory // len(order)
    most = max(1, PAIRS_PER_STEP * 128 // memory)
    step = max(d for d in range(1, most + 1) if all(x % d == 0 for x in (pairs, offset)))
    block = step * LANES

    def body(*refs):
        q_ref, do_ref, ka_ref, kb_ref, va_ref, vb_ref, fa_ref, fb_ref = refs[:8]
        att_ref, dq_ref, lo_ref, hi_ref = refs[-4:]
        flags = jnp.concatenate([fa_ref[...], fb_ref[...]], axis=0).astype(F32)
        flags = jnp.concatenate([flags[at * rows : (at + 1) * rows, :1] for at in order], axis=0)
        bias = jnp.where(flags > 0, 0.0, NEG)
        left = lax.broadcasted_iota(jnp.int32, (memory, LANES), 1) < HEAD_DIM
        zero = jnp.zeros((memory, LANES), BF16)

        def both(x):
            return jnp.concatenate([jnp.where(left, x, zero), jnp.where(left, zero, x)], axis=0)

        pair = [{} for _ in range(step)]
        cols = [pl.ds(i * LANES, LANES) for i in range(step)]

        def scores(i):
            k = jnp.concatenate([ka_ref[:, cols[i]], kb_ref[:, cols[i]]], axis=0) * jnp.asarray(SCALE, BF16)
            v = jnp.concatenate([va_ref[:, cols[i]], vb_ref[:, cols[i]]], axis=0)
            pair[i].update(k=both(k), v=both(v))
            pair[i]["s"] = dot(pair[i]["k"], q_ref[:, cols[i]], 1, 1).reshape(2, memory, tokens) + bias
            pair[i]["grad_p"] = dot(pair[i]["v"], do_ref[:, cols[i]], 1, 1).reshape(2, memory, tokens)

        def softmax(i):
            s = pair[i].pop("s")
            e = jnp.exp(s - jnp.max(s, axis=1, keepdims=True))
            pair[i]["p"] = e * (1.0 / jnp.sum(e, axis=1, keepdims=True))
            pair[i]["p_low"] = pair[i]["p"].astype(BF16).reshape(2 * memory, tokens)

        def attended(i):
            pair[i]["att"] = dot(pair[i]["v"], pair[i]["p_low"], 0, 0).astype(BF16)
            dv = dot(pair[i].pop("p_low"), do_ref[:, cols[i]], 1, 0)
            store(2 * i + 1, jnp.where(left, dv[:memory], dv[memory:]))

        def score_grads(i):
            att = pair[i].pop("att")
            delta = (do_ref[:, cols[i]].T.astype(F32) * att.astype(F32)).reshape(2, HEAD_DIM, tokens)
            delta = jnp.sum(delta, axis=1, keepdims=True)
            grad_s = pair[i].pop("p") * (pair[i].pop("grad_p") - delta)
            pair[i]["grad_s"] = grad_s.astype(BF16).reshape(2 * memory, tokens)
            att_ref[:, cols[i]] = att.T

        def grads(i):
            dq_ref[:, cols[i]] = dot(pair[i]["k"], pair[i]["grad_s"], 0, 0).astype(BF16).T
            dk = dot(pair[i]["grad_s"], q_ref[:, cols[i]], 1, 0)
            store(2 * i, jnp.where(left, dk[:memory], dk[memory:]) * SCALE)

        def store(j, x):
            c = pl.ds(j * LANES, LANES)
            lo_ref[:, c] = x[:half]
            hi_ref[:, c] = x[half:]

        stages = (scores, softmax, attended, score_grads, grads)
        for t in range(step + len(stages) - 1):
            for j, stage in enumerate(stages):
                if 0 <= t - j < step:
                    stage(t - j)

    def columns(rows, width, start):
        return pl.BlockSpec((rows, width), lambda g: (0, g + start))

    token_spec = columns(tokens, block, offset // step)
    k_spec = columns(half, block, 0)
    v_spec = columns(half, block, pairs // step)
    flag_spec = pl.BlockSpec((half, LANES), lambda g: (0, live[0].shape[1] // LANES - 1))
    term_spec = columns(half, 2 * block, 0)
    extra = results or ()
    scratch = min(52, 12 + step * memory * tokens * 2 * 4 * 4 // 2**20)
    return pl.pallas_call(
        body,
        grid=(pairs // step,),
        in_specs=[token_spec, token_spec, k_spec, k_spec, v_spec, v_spec, flag_spec, flag_spec]
        + [pl.BlockSpec(memory_space=pl.ANY)] * len(extra),
        out_specs=[token_spec, token_spec, term_spec, term_spec],
        out_shape=[jax.ShapeDtypeStruct((tokens, width), BF16)] * 2
        + [jax.ShapeDtypeStruct((half, 2 * pairs * LANES), F32)] * 2,
        input_output_aliases={8 + i: i for i in range(len(extra))},
        compiler_params=pltpu.CompilerParams(
            dimension_semantics=("arbitrary",), vmem_limit_bytes=scratch * 2**20
        ),
        cost_estimate=pl.CostEstimate(
            flops=pairs * 12 * tokens * 2 * memory * LANES,
            transcendentals=pairs * tokens * 2 * memory,
            bytes_accessed=pairs * LANES * 8 * (tokens + 2 * memory),
        ),
    )(queries, dout, first, second, first, second, *live, *extra)


def split_pairs(total):
    chunks, done, share = [], 0, 0.0
    for part, turn in CHUNKS:
        share += part
        end = min(total, round(share * total))
        if end > done:
            chunks.append((done, end - done, turn))
        done = end
    assert done == total
    return chunks


def solution(mesh):
    n = mesh.shape["ctx"]
    bits = [1 << b for b in range(n.bit_length() - 1)]
    assert n == 1 << len(bits)

    def reduce_order(turn):
        order = list(bits)
        if turn and len(order) > 2:
            order[1], order[2] = order[2], order[1]
        return order

    def swap(x, bit):
        return lax.ppermute(x, "ctx", [(i, i ^ bit) for i in range(n)])

    def gather(chunks, orders):
        chunks = list(chunks)
        for step in range(len(bits) - 1):
            before = None
            for k, order in enumerate(orders):
                received = swap(chunks[k], order[step])
                if before is not None:
                    received, _ = lax.optimization_barrier((received, before))
                chunks[k] = before = jnp.concatenate([chunks[k], received], axis=0)
        return [(x, swap(x, order[-1])) for x, order in zip(chunks, orders)]

    def places(order):
        return [sum(b for i, b in enumerate(order) if j >> i & 1) for j in range(n)]

    def scatter(keep, send, order):
        x = keep + swap(send, order[0])
        for bit in order[1:]:
            half = x.shape[0] // 2
            x = x[:half] + swap(x[half:], bit)
        return x

    def per_device(queries, keys, values, lengths, dout):
        rows, width = keys.shape
        chunks = split_pairs(width // LANES)
        orders = [reduce_order(turn) for _, _, turn in chunks]
        live = lax.broadcasted_iota(jnp.int32, (rows, LANES), 0) < lengths[0]
        packed = []
        for start, pairs, _ in chunks:
            cols = slice(start * LANES, (start + pairs) * LANES)
            parts = [keys[:, cols], values[:, cols]] + ([] if packed else [live.astype(BF16)])
            packed.append(jnp.concatenate(parts, axis=1))
        gathered = gather(packed, [order[::-1] for order in orders])
        flag_places = places(orders[0][::-1])
        results, sums = None, []
        for (start, pairs, _), order, (first, second) in zip(chunks, orders, gathered):
            tokens = (queries, dout)
            if not start:
                tokens = [pltpu.with_memory_space_constraint(x, pltpu.MemorySpace.HBM) for x in tokens]
            at = [flag_places.index(p) for p in places(order[::-1])]
            out = attention(*tokens,  first, second, gathered[0], at, results, start, pairs)
            results = out[:2]
            sums.append(scatter(*out[2:], order))
        total = jnp.concatenate(sums, axis=1).reshape(rows, width // LANES, 2, LANES)
        key_grad = total[:, :, 0].reshape(rows, width).astype(BF16)
        value_grad = total[:, :, 1].reshape(rows, width).astype(BF16)
        return (*results, key_grad, value_grad)

    spec = P(("groups", "ctx"), None)
    return jax.shard_map(
        per_device,
        mesh=mesh,
        in_specs=(spec, spec, spec, P(("groups", "ctx")), spec),
        out_specs=(spec,) * 4,
        check_vma=False,
    )
```
